32 devices in a mesh: cond: 4 (over y, x), space: 8 (over z, core).
Axes of the slice: x: 2, y: 2, z: 4, core: 2. Of those that a mesh axis runs over, the one named last changes fastest.
Arguments:
- flow: float32 [8, 3, 128, 2048], P('cond', None, 'space'), may hold values from -4 to 4
- forcing: float32 [8, 2, 128, 2048], P('cond', None, 'space'), may hold values from -4 to 4
- wet: int32 [8, 128, 2048], P('cond', 'space'), may hold values 0 or 1
- depth: float32 [128, 2048], P('space'), may hold values from 0.5 to 2
- limiter: int32 [128, 2048], P('space'), may hold values 0 or 1
- weights: int32 [8], replicated, may hold values from 1 to 9
- bed: float32 [128, 2048], P('space'), may hold values from -6 to 6
- diffusivity: float32 [128, 2048], P('space'), may hold values from 0.2 to 5
Outputs:
- surface: float32 [8, 128, 2048], P('cond', 'space')
- bed_new: float32 [128, 2048], P('space')
The draws below stay inside these ranges and needn't reach their ends.
All inputs are finite; a program needn't handle non-finite values. No bound on the sum of `wet` or of `limiter` on one device may be relied on, other than what follows from the above.
Results may differ from the reference program's by a relative error of at most 0.0001.
Values sent between devices are 32-bit elements; how exact they have to be, the bound alone decides.
No kernel may reach another device: no remote copies, remote signals or barrier semaphores. Data moves between devices by JAX's collectives and lax.ppermute only.
A program may use at most 64 MiB of HBM per device.

```python
import math
import jax
import jax.numpy as jnp
from jax import lax

NY = 2048
STEPS = 4
ITERS = 2
NX = 128
CONDS = 8


def set_ends(drawn, stream_key, smallest, high):
    extent = drawn.shape
    place = [jax.random.randint(jax.random.fold_in(stream_key, axis), (), 0, extent[axis]) for axis in range(len(extent))]
    drawn = drawn.at[tuple(place)].set(smallest)
    longest = extent.index(max(extent))
    place[longest] = (place[longest] + 1) % extent[longest]
    return drawn.at[tuple(place)].set(high)


def block_scale(stream_key, shape, pieces, smallest, largest):
    level, own = 1.0, jax.random.fold_in(stream_key, 6)
    for axis_at, blocks in pieces:
        draws = jnp.exp(jax.random.uniform(jax.random.fold_in(own, axis_at), (blocks,), jnp.float32, smallest / len(pieces), largest / len(pieces)))
        level = level * jnp.repeat(draws, shape[axis_at] // blocks).reshape([-1 if axis == axis_at else 1 for axis in range(len(shape))])
    return level


def gaussian(stream_key, shape, scale, reach, pieces=(), dtype=jnp.bfloat16):
    values = scale * jax.random.normal(stream_key, shape, jnp.float32)
    if pieces:
        values = values * block_scale(stream_key, shape, pieces, -0.22, 0.18)
    return jnp.clip(values, -reach, reach).astype(dtype)


def setup_inputs(seed: int = 0) -> dict:
    streams_of = jax.random.split(jax.random.key(seed), 9)
    flow = gaussian(streams_of[0], (CONDS, 3, NX, NY), 0.5, 4.0, ((0, 4), (2, 8)), jnp.float32)
    forcing = gaussian(streams_of[1], (CONDS, 2, NX, NY), 0.5, 4.0, ((0, 4), (2, 8)), jnp.float32)
    wet = set_ends((jax.random.randint(streams_of[2], (CONDS, NX, NY), 0, 8) < 7).astype(jnp.int32), jax.random.fold_in(streams_of[2], 1), 0, 1)
    depth = jnp.clip(jnp.exp(math.log(2.0) - 1.3862944 * jax.random.uniform(streams_of[3], (NX, NY), jnp.float32) ** block_scale(streams_of[3], (NX, NY), ((0, 8),), -0.2, 0.2)), 0.5, 2.0)
    limiter = set_ends((jax.random.randint(streams_of[4], (NX, NY), 0, 2) < 1).astype(jnp.int32), jax.random.fold_in(streams_of[4], 1), 0, 1)
    weights = set_ends(jax.random.randint(streams_of[5], (CONDS,), 1, 10), jax.random.fold_in(streams_of[5], 1), 1, 9).astype(jnp.int32)
    bed = gaussian(streams_of[6], (NX, NY), 1.0, 6.0, ((0, 8),), jnp.float32)
    diffusivity = jnp.clip(jnp.exp(math.log(5.0) - 3.218876 * jax.random.uniform(streams_of[7], (NX, NY), jnp.float32) ** block_scale(streams_of[7], (NX, NY), ((0, 8),), -0.2, 0.2)), 0.2, 5.0)
    return dict(flow=flow, forcing=forcing, wet=wet, depth=depth, limiter=limiter, weights=weights, bed=bed, diffusivity=diffusivity)


time_step = 0.4
gravity = 1.0
friction = 0.1
transport_base = 0.5
morph_factor = 1.0
slope_coeff = 1.0


def row_diff(field):
    padded = jnp.pad(field, ((1, 1), (0, 0)))
    return 0.5 * (padded[2:] - padded[:-2])


def column_diff(field):
    padded = jnp.pad(field, ((0, 0), (1, 1)))
    return 0.5 * (padded[:, 2:] - padded[:, :-2])


def tendency(state_now, depth, wet_mask, force):
    elevation, vel_first, vel_second = state_now[0], state_now[1], state_now[2]
    rate_elev = -(row_diff(depth * vel_first) + column_diff(depth * vel_second))
    rate_first = -gravity * row_diff(elevation) - friction * vel_first + force[0]
    rate_second = -gravity * column_diff(elevation) - friction * vel_second + force[1]
    return wet_mask * jnp.stack([rate_elev, rate_first, rate_second])


def transport(state_now, limit_mask):
    vel_first, vel_second = state_now[1], state_now[2]
    energy = vel_first * vel_first + vel_second * vel_second
    factor = (transport_base + energy) / (1.0 + limit_mask * energy)
    return vel_first * factor, vel_second * factor


def neighbours(padded):
    return [padded[:-2, 1:-1], padded[2:, 1:-1], padded[1:-1, :-2], padded[1:-1, 2:]]


def apply_op(field, coefs):
    near = neighbours(jnp.pad(field, 1))
    total = coefs[0] * (field - near[0]) + coefs[1] * (field - near[1])
    total = total + coefs[2] * (field - near[2]) + coefs[3] * (field - near[3])
    return field + slope_coeff * total


def reference(flow, forcing, wet, depth, limiter, weights, bed, diffusivity):
    limit_mask = limiter.astype(jnp.float32)

    def one_condition(items):
        state_now, force, wet_int = items
        wet_mask = wet_int.astype(jnp.float32)[None]
        bed_change = jnp.zeros(state_now.shape[1:], jnp.float32)
        for stepper in range(STEPS):
            first_section = state_now + time_step * tendency(state_now, depth, wet_mask, force)
            state_now = 0.5 * (state_now + first_section + time_step * tendency(first_section, depth, wet_mask, force))
            flux_first, flux_second = transport(state_now, limit_mask)
            bed_change = bed_change - morph_factor * (row_diff(flux_first) + column_diff(flux_second))
        return state_now[0], bed_change

    surface, changes = lax.map(one_condition, (flow, forcing, wet))
    weight_all = weights.astype(jnp.float32)
    increment = jnp.sum(weight_all[:, None, None] * changes, 0) / jnp.sum(weight_all)
    padded = jnp.pad(diffusivity, 1)
    centre = padded[1:-1, 1:-1]
    coefs = [centre * other / (centre + other) for other in neighbours(padded)]
    rhs = bed + increment
    solution = jnp.zeros_like(rhs)
    residual = rhs
    direction = rhs
    norm_now = jnp.sum(rhs * rhs)
    for sweep in range(ITERS):
        image = apply_op(direction, coefs)
        alpha = norm_now / jnp.sum(direction * image)
        solution = solution + alpha * direction
        if sweep + 1 < ITERS:
            residual = residual - alpha * image
            norm_next = jnp.sum(residual * residual)
            direction = residual + (norm_next / norm_now) * direction
            norm_now = norm_next
    return surface, solution
```

```python
import functools

import jax
import jax.numpy as jnp
from jax import lax
from jax.experimental import pallas as pl
from jax.experimental.pallas import tpu as pltpu
from jax.sharding import PartitionSpec as P

STEPS = 4

time_step = 0.4
gravity = 1.0
friction = 0.1
transport_base = 0.5
morph_factor = 1.0
slope_coeff = 1.0

LANES = 128
ABOVE, BELOW = 1, 2
DEEP = 2 * STEPS + BELOW + 1
NEXT = DEEP - 1
OWN = 24
FLUX_ROWS = BELOW + 1

FLOW = ("elev", "first", "second", "force_a", "force_b", "wet")
HALO = dict(
    elev=DEEP, first=DEEP, depth=DEEP, second=NEXT, force_a=NEXT, force_b=NEXT, wet=NEXT,
    limiter=FLUX_ROWS, bed=BELOW, diffusivity=BELOW,
)
MESSAGE = (FLOW + ("depth", "limiter"), FLOW + ("bed", "diffusivity"))


def offsets(names, tiles):
    places, at = {}, 0
    for name in names:
        places[name] = at
        at += tiles * HALO[name]
    return places, at


def lanes_of(tile):
    return pl.ds(pl.multiple_of(tile * LANES, LANES), LANES)


def own_rows(refs, name, rows, tile):
    if name in ("elev", "first", "second"):
        return refs["flow"][0, ("elev", "first", "second").index(name), rows, lanes_of(tile)]
    if name in ("force_a", "force_b"):
        return refs["forcing"][0, ("force_a", "force_b").index(name), rows, lanes_of(tile)]
    if name == "wet":
        return refs["wet"][0, rows, lanes_of(tile)].astype(jnp.float32)
    return refs[name][rows, lanes_of(tile)].astype(jnp.float32)


def pack_kernel(names, keys, place_ref, *args):
    refs, (across_ref, chip_ref) = dict(zip(keys, args)), args[len(keys) :]
    height, tiles = refs[keys[-1]].shape[-2], refs[keys[-1]].shape[-1] // LANES
    places, _ = offsets(names, tiles)

    def fill(head_ref, tail_ref):
        def body(tile, carry):
            for name in names:
                count = HALO[name]
                where = pl.ds(places[name] + tile * count, count)
                head_ref[where, :] = own_rows(refs, name, slice(0, count), tile)
                tail_ref[where, :] = own_rows(refs, name, slice(height - count, height), tile)
            return carry

        lax.fori_loop(0, tiles, body, 0)

    odd = place_ref[1]

    @pl.when(odd == 0)
    def _():
        fill(across_ref, chip_ref)

    @pl.when(odd == 1)
    def _():
        fill(chip_ref, across_ref)


def beside(field, tile, rows, centre):
    lane = lax.broadcasted_iota(jnp.int32, centre.shape, 1)
    left = pltpu.roll(jnp.where(lane == LANES - 1, field[tile - 1, rows, :], centre), 1, 1)
    right = pltpu.roll(jnp.where(lane == 0, field[tile + 1, rows, :], centre), LANES - 1, 1)
    return left, right


def spread(dst, name, tile, own, head, tail, places, height, base):
    count = HALO[name]
    where = pl.ds(places[name] + tile * count, count)
    dst[tile + 1, base - count : base, :] = head[where, :]
    for row in range(0, height, 8):
        dst[tile + 1, base + row : base + row + 8, :] = own_rows(own, name, slice(row, row + 8), tile)
    dst[tile + 1, base + height : base + height + count, :] = tail[where, :]


def flow_kernel(which, keys, place_ref, weights_ref, *args):
    refs = dict(zip(keys, args))
    n_in = len(keys)
    surface_ref, low_ref, high_ref = args[n_in : n_in + 3]
    names = ("elev", "first", "second", "elev1", "first1", "second1", "wet", "keep", "depth_wet",
             "force_a", "force_b", "depth", "limiter", "flux_a", "flux_b")
    buf = dict(zip(names, args[n_in + 3 :]))
    height, tiles = refs["depth"].shape[0], refs["depth"].shape[1] // LANES
    flow_places, _ = offsets(MESSAGE[which], tiles)
    static_places, _ = offsets(MESSAGE[0], tiles)
    span = buf["elev"].shape[1]

    for name in ("elev", "second", "elev1", "second1", "flux_b"):
        zero = jnp.zeros((span, LANES), jnp.float32)
        buf[name][0, :, :] = zero
        buf[name][tiles + 1, :, :] = zero

    first_tile = (OWN - DEEP) // 8
    last_tile = -(-(OWN + height + DEEP) // 8)

    def load(head, tail, static_head, static_tail):
        def body(tile, carry):
            for name in FLOW:
                spread(buf[name], name, tile, refs, head, tail, flow_places, height, OWN)
            for name in ("depth", "limiter"):
                spread(buf[name], name, tile, refs, static_head, static_tail, static_places, height, OWN)
            at = tile + 1
            for row in range(8 * first_tile, 8 * last_tile, 8):
                rows = slice(row, row + 8)
                wet, depth = buf["wet"][at, rows, :], buf["depth"][at, rows, :]
                half = (0.5 * time_step) * wet
                depth_wet = depth * half
                buf["first"][at, rows, :] = depth * buf["first"][at, rows, :]
                buf["second"][at, rows, :] = depth * buf["second"][at, rows, :]
                buf["force_a"][at, rows, :] = 2.0 * depth_wet * buf["force_a"][at, rows, :]
                buf["force_b"][at, rows, :] = 2.0 * depth_wet * buf["force_b"][at, rows, :]
                buf["wet"][at, rows, :] = half
                buf["keep"][at, rows, :] = 1.0 - (2.0 * friction) * half
                buf["depth_wet"][at, rows, :] = gravity * depth_wet
                buf["depth"][at, rows, :] = jnp.where(depth > 0.0, 1.0 / depth, 0.0)
            return carry

        lax.fori_loop(0, tiles, body, 0)

    odd = place_ref[1]

    @pl.when(odd == 0)
    def _():
        load(refs["across"], refs["chip"], refs["static_across"], refs["static_chip"])

    @pl.when(odd == 1)
    def _():
        load(refs["chip"], refs["across"], refs["static_chip"], refs["static_across"])

    def section(number):
        second = number % 2 == 0
        source = ("elev1", "first1", "second1") if second else ("elev", "first", "second")
        target = ("elev", "first", "second") if second else ("elev1", "first1", "second1")
        elev, first, vert = (buf[name] for name in source)
        begin = (OWN - DEEP + 1 + number) // 8
        end = -(-(OWN + height + DEEP - number) // 8)
        flux_begin = (OWN - FLUX_ROWS + 1) // 8
        flux_end = -(-(OWN + height + FLUX_ROWS) // 8)
        last = number == 2 * STEPS

        def body(tile, carry):
            at = tile + 1
            for block in range(begin, end):
                row = 8 * block
                rows, up, down = slice(row, row + 8), slice(row - 1, row + 7), slice(row + 1, row + 9)
                e, f, s = elev[at, rows, :], first[at, rows, :], vert[at, rows, :]
                e_left, e_right = beside(elev, at, rows, e)
                s_left, s_right = beside(vert, at, rows, s)
                keep, depth_wet = buf["keep"][at, rows, :], buf["depth_wet"][at, rows, :]
                gone = (first[at, down, :] - first[at, up, :]) + (s_right - s_left)
                new_e = e - buf["wet"][at, rows, :] * gone
                new_f = (keep * f + buf["force_a"][at, rows, :]) - depth_wet * (elev[at, down, :] - elev[at, up, :])
                new_s = (keep * s + buf["force_b"][at, rows, :]) - depth_wet * (e_right - e_left)
                if second:
                    new_e = 0.5 * (buf["elev"][at, rows, :] + new_e)
                    new_f = 0.5 * (buf["first"][at, rows, :] + new_f)
                    new_s = 0.5 * (buf["second"][at, rows, :] + new_s)
                if not last:
                    buf[target[0]][at, rows, :] = new_e
                    buf[target[1]][at, rows, :] = new_f
                    buf[target[2]][at, rows, :] = new_s
                elif 0 <= row - OWN < height:
                    surface_ref[0, row - OWN : row - OWN + 8, lanes_of(tile)] = new_e
                if second and flux_begin <= block < flux_end:
                    inverse = buf["depth"][at, rows, :]
                    vel_a, vel_b = new_f * inverse, new_s * inverse
                    energy = vel_a * vel_a + vel_b * vel_b
                    factor = (transport_base + energy) / (1.0 + buf["limiter"][at, rows, :] * energy)
                    flux_a, flux_b = vel_a * factor, vel_b * factor
                    if number > 2:
                        flux_a = buf["flux_a"][at, rows, :] + flux_a
                        flux_b = buf["flux_b"][at, rows, :] + flux_b
                    buf["flux_a"][at, rows, :] = flux_a
                    buf["flux_b"][at, rows, :] = flux_b
            return carry

        lax.fori_loop(0, tiles, body, 0)

    for number in range(1, 2 * STEPS + 1):
        section(number)

    total = weights_ref[0]
    for other in range(1, weights_ref.shape[0]):
        total = total + weights_ref[other]
    scale = jnp.full((8, LANES), weights_ref[place_ref[0] + which], jnp.int32).astype(jnp.float32)
    scale = (-0.5 * morph_factor) * scale / jnp.full((8, LANES), total, jnp.int32).astype(jnp.float32)
    reach = height + ABOVE + BELOW
    begins = list(range(0, reach - 7, 8))
    if begins[-1] + 8 < reach:
        begins.append(reach - 8)

    def emit(out_ref, before, start):
        def body(local_tile, carry):
            at = start + local_tile + 1
            for begin in begins:
                row = OWN - ABOVE + begin
                rows, up, down = slice(row, row + 8), slice(row - 1, row + 7), slice(row + 1, row + 9)
                flux_b = buf["flux_b"][at, rows, :]
                left, right = beside(buf["flux_b"], at, rows, flux_b)
                change = (buf["flux_a"][at, down, :] - buf["flux_a"][at, up, :]) + (right - left)
                where = pl.ds(local_tile * reach + begin, 8)
                piece = scale * change
                if before is not None:
                    piece = before[where, :] + piece
                out_ref[where, :] = piece
            return carry

        lax.fori_loop(0, tiles // 2, body, 0)

    emit(low_ref, refs.get("low"), 0)
    emit(high_ref, refs.get("high"), tiles // 2)


def moment_kernel(keys, place_ref, *args):
    refs = dict(zip(keys, args))
    n_in = len(keys)
    rhs_ref, image_ref, moments_ref, field, diffuse, image, down_k, right_k = args[n_in:]
    height, tiles = refs["bed"].shape[0], refs["bed"].shape[1] // LANES
    places, _ = offsets(MESSAGE[1], tiles)
    base = 8
    reach = height + ABOVE + BELOW
    span = field.shape[1]
    for scratch in (field, diffuse, image):
        zero = jnp.zeros((span, LANES), jnp.float32)
        scratch[0, :, :] = zero
        scratch[tiles + 1, :, :] = zero

    def load(head, tail):
        def fill(tile, carry):
            spread(field, "bed", tile, refs, head, tail, places, height, base)
            spread(diffuse, "diffusivity", tile, refs, head, tail, places, height, base)
            return carry

        lax.fori_loop(0, tiles, fill, 0)

    odd = place_ref[1]

    @pl.when(odd == 0)
    def _():
        load(refs["across"], refs["chip"])

    @pl.when(odd == 1)
    def _():
        load(refs["chip"], refs["across"])

    def add(mine, other, start):
        def body(local_tile, carry):
            where = pl.ds(local_tile * reach, reach)
            rows = slice(base - ABOVE, base - ABOVE + reach)
            at = start + local_tile + 1
            field[at, rows, :] = field[at, rows, :] + (mine[where, :] + other[where, :])
            return carry

        lax.fori_loop(0, tiles // 2, body, 0)

    add(refs["low"], refs["low_other"], 0)
    add(refs["high"], refs["high_other"], tiles // 2)

    def face(here, there):
        both = here + there
        return jnp.where(both > 0.0, slope_coeff * here * there / both, 0.0)

    def apply(tile, carry):
        at = tile + 1
        square, first = carry
        for row in range(base, base + height + 8, 8):
            rows, up, down = slice(row, row + 8), slice(row - 1, row + 7), slice(row + 1, row + 9)
            d, x = diffuse[at, rows, :], field[at, rows, :]
            d_left, d_right = beside(diffuse, at, rows, d)
            x_left, x_right = beside(field, at, rows, x)
            k_down, k_right = face(d, diffuse[at, down, :]), face(d, d_right)
            gap_down, gap_right = x - field[at, down, :], x - x_right
            flow_down, flow_right = k_down * gap_down, k_right * gap_right
            result = (flow_down + face(d, diffuse[at, up, :]) * (x - field[at, up, :])) + (
                flow_right + face(d, d_left) * (x - x_left)
            )
            image[at, rows, :] = result
            down_k[at, rows, :] = k_down
            right_k[at, rows, :] = k_right
            if row < base + height:
                rhs_ref[tile, row - base : row - base + 8, :] = x
                image_ref[tile, row - base : row - base + 8, :] = result
                square = square + x * x
                first = first + (flow_down * gap_down + flow_right * gap_right)
        return square, first

    zero = jnp.zeros((8, LANES), jnp.float32)
    square, first = lax.fori_loop(0, tiles, apply, (zero, zero))

    def again(tile, carry):
        at = tile + 1
        second, third = carry
        lane = lax.broadcasted_iota(jnp.int32, (8, LANES), 1)
        for row in range(base, base + height, 8):
            rows, down = slice(row, row + 8), slice(row + 1, row + 9)
            w = image[at, rows, :]
            w_right = pltpu.roll(jnp.where(lane == 0, image[at + 1, rows, :], w), LANES - 1, 1)
            gap_down, gap_right = w - image[at, down, :], w - w_right
            second = second + w * w
            third = third + (
                down_k[at, rows, :] * gap_down * gap_down + right_k[at, rows, :] * gap_right * gap_right
            )
        return second, third

    second, third = lax.fori_loop(0, tiles, again, (zero, zero))
    for slot, value in enumerate((square, first, second, third)):
        moments_ref[slot : slot + 1, :] = jnp.sum(value, axis=0, keepdims=True)
    moments_ref[4:8, :] = jnp.zeros((4, LANES), jnp.float32)


def final_kernel(rhs_ref, image_ref, *args):
    moments, (out_ref,) = args[:-1], args[-1:]
    total = moments[0][...]
    for part in moments[1:]:
        total = total + part[...]
    total = jnp.sum(total, axis=1, keepdims=True)
    norm, first, second, third = (total[slot : slot + 1, :] for slot in range(4))
    alpha = norm / (norm + first)
    theta = first / norm
    spread_ = second - theta * first
    curve = third - 2.0 * theta * second + theta * theta * first
    ratio = alpha * alpha * spread_ / norm
    beta = spread_ / (spread_ + curve - alpha * spread_ * (spread_ / norm))
    on_rhs = jnp.broadcast_to(alpha + beta * (alpha * theta + ratio), (8, LANES))
    on_image = jnp.broadcast_to(beta * alpha, (8, LANES))
    tiles, height = rhs_ref.shape[:2]

    def body(tile, carry):
        for row in range(0, height, 8):
            rows = slice(row, row + 8)
            out_ref[rows, lanes_of(tile)] = on_rhs * rhs_ref[tile, rows, :] - on_image * image_ref[tile, rows, :]
        return carry

    lax.fori_loop(0, tiles, body, 0)


def whole(shape):
    return pl.BlockSpec(shape, lambda *_: (0,) * len(shape))


def picked(shape, which):
    return pl.BlockSpec((1,) + shape[1:], lambda *_: (which,) + (0,) * (len(shape) - 1))


SMEM = pl.BlockSpec(memory_space=pltpu.SMEM)
PARAMS = dict(vmem_limit_bytes=48 * 1024 * 1024)


def cost(flops, moved):
    return pl.CostEstimate(flops=flops, bytes_accessed=moved, transcendentals=0)


def swap_chip(x, count):
    return lax.ppermute(x, "space", [(i, i ^ 1) for i in range(count)])


def swap_across(x, count):
    pairs = [(i, i + 1) for i in range(1, count - 1, 2)]
    return lax.ppermute(x, "space", pairs + [(b, a) for a, b in pairs])


def phases_of(count):
    bits = [1 << k for k in range(count.bit_length() - 1)]
    out = [bits[:1]]
    for k in range(1, len(bits), 2):
        pair = bits[k : k + 2]
        out.append([pair[0]] if len(pair) == 1 else [pair[0], pair[1], pair[0] + pair[1]])
    return out


def local(flow, forcing, wet, depth, limiter, weights, bed, diffusivity):
    here, _, height, width = flow.shape
    tiles = width // LANES
    strips, groups = lax.axis_size("space"), lax.axis_size("cond")
    place = jnp.stack([lax.axis_index("cond") * here, lax.axis_index("space") % 2]).astype(jnp.int32)
    static = dict(depth=depth, limiter=limiter, bed=bed, diffusivity=diffusivity)
    reach = height + ABOVE + BELOW

    across, chip = [], []
    for which in range(here):
        names = MESSAGE[which]
        keys = ("flow", "forcing", "wet") + names[len(FLOW) :]
        arrays = dict(flow=flow, forcing=forcing, wet=wet, **static)
        size = offsets(names, tiles)[1]
        shape = jax.ShapeDtypeStruct((size, LANES), jnp.float32)
        out = pl.pallas_call(
            functools.partial(pack_kernel, names, keys),
            out_shape=(shape, shape),
            grid=(1,),
            in_specs=[SMEM] + [picked(arrays[k].shape, which) if k in ("flow", "forcing", "wet") else whole(arrays[k].shape) for k in keys],
            out_specs=(whole(shape.shape), whole(shape.shape)),
            compiler_params=pltpu.CompilerParams(**PARAMS),
            cost_estimate=cost(1000, 6 * height * width * 4 + size * LANES * 8),
            name=f"pack{which}",
        )(place, *(arrays[k] for k in keys))
        across.append(swap_across(out[0], strips))
        chip.append(swap_chip(out[1], strips))

    surface_shape = jax.ShapeDtypeStruct((here, height, width), jnp.float32)
    half_shape = jax.ShapeDtypeStruct((tiles // 2 * reach, LANES), jnp.float32)
    surface = low = high = None
    for which in range(here):
        arrays = dict(flow=flow, forcing=forcing, wet=wet, depth=depth, limiter=limiter)
        specs = {k: picked(v.shape, which) if k in ("flow", "forcing", "wet") else whole(v.shape) for k, v in arrays.items()}
        arrays.update(across=across[which], chip=chip[which], static_across=across[0], static_chip=chip[0])
        aliases = {}
        if which:
            arrays.update(low=low, high=high)
        for k in arrays:
            specs.setdefault(k, whole(arrays[k].shape))
        if which:
            arrays["surface"] = surface
            specs["surface"] = pl.BlockSpec(memory_space=pl.ANY)
            aliases = {2 + len(arrays) - 1: 0}
        keys = tuple(arrays)
        surface, low, high = pl.pallas_call(
            functools.partial(flow_kernel, which, keys),
            out_shape=(surface_shape, half_shape, half_shape),
            grid=(1,),
            in_specs=[SMEM, SMEM] + [specs[k] for k in keys],
            out_specs=(picked(surface_shape.shape, which), whole(half_shape.shape), whole(half_shape.shape)),
            scratch_shapes=[pltpu.VMEM((tiles + 2, 64, LANES), jnp.float32)] * 15,
            input_output_aliases=aliases,
            compiler_params=pltpu.CompilerParams(**PARAMS),
            cost_estimate=cost(2 * STEPS * 40 * 40 * width, 8 * height * width * 4),
            name=f"flow{which}",
        )(place, weights, *(arrays[k] for k in keys))

    bits = [1 << k for k in range(groups.bit_length() - 1)]
    for k, bit in enumerate(bits):
        low_other = lax.ppermute(low, "cond", [(i, i ^ bit) for i in range(groups)])
        flip = bits[-1 - k]
        high_other = lax.ppermute(high, "cond", [(i, i ^ flip) for i in range(groups)])
        if k + 1 < len(bits):
            low, high = low + low_other, high + high_other

    arrays = dict(low=low, low_other=low_other, high=high, high_other=high_other, bed=bed, diffusivity=diffusivity, across=across[1], chip=chip[1])
    block = jax.ShapeDtypeStruct((tiles, height, LANES), jnp.float32)
    small = jax.ShapeDtypeStruct((8, LANES), jnp.float32)
    rhs, image, moments = pl.pallas_call(
        functools.partial(moment_kernel, tuple(arrays)),
        out_shape=(block, block, small),
        grid=(1,),
        in_specs=[SMEM] + [whole(v.shape) for v in arrays.values()],
        out_specs=(whole(block.shape), whole(block.shape), whole(small.shape)),
        scratch_shapes=[pltpu.VMEM((tiles + 2, height + 24, LANES), jnp.float32)] * 5,
        compiler_params=pltpu.CompilerParams(**PARAMS),
        cost_estimate=cost(60 * height * width, 8 * height * width * 4),
        name="moments",
    )(place, *arrays.values())

    phases = phases_of(strips)
    for k, phase in enumerate(phases):
        others = [lax.ppermute(moments, "space", [(i, i ^ m) for i in range(strips)]) for m in phase]
        if k + 1 < len(phases):
            for other in others:
                moments = moments + other

    terms = [moments] + others
    bed_new = pl.pallas_call(
        final_kernel,
        out_shape=jax.ShapeDtypeStruct((height, width), jnp.float32),
        grid=(1,),
        in_specs=[whole(rhs.shape), whole(image.shape)] + [whole(small.shape)] * len(terms),
        out_specs=whole((height, width)),
        compiler_params=pltpu.CompilerParams(**PARAMS),
        cost_estimate=cost(3 * height * width, 3 * height * width * 4),
        name="final",
    )(rhs, image, *terms)
    return (surface, bed_new)


def solution(mesh):
    in_specs = (
        P("cond", None, "space", None),
        P("cond", None, "space", None),
        P("cond", "space", None),
        P("space", None),
        P("space", None),
        P(),
        P("space", None),
        P("space", None),
    )
    out_specs = (P("cond", "space", None), P("space", None))
    return jax.shard_map(local, mesh=mesh, in_specs=in_specs, out_specs=out_specs, check_vma=False)
```

```python
import functools

import jax
import jax.numpy as jnp
from jax import lax
from jax.experimental import pallas as pl
from jax.experimental.pallas import tpu as pltpu
from jax.sharding import PartitionSpec as P

STEPS = 4

time_step = 0.4
gravity = 1.0
friction = 0.1
transport_base = 0.5
morph_factor = 1.0
slope_coeff = 1.0

LANES = 128
(
    ELEV, FIRST, SECOND, FORCE_A, FORCE_B, HALF, KEEP, WET_DEPTH, KEEP_AHEAD, WET_AHEAD, INVERSE, LIMITER,
    ELEV_MID, FIRST_MID, SECOND_MID, DEPTH, FLUX_A, FLUX_B, BED, DIFFUSIVITY, FLOW_IN, FORCING, WET,
    ACROSS, CHIP, STATIC_ACROSS, STATIC_CHIP, LOW, HIGH, LOW_OTHER, HIGH_OTHER, SURFACE, BASE, DERIVED,
) = range(34)

ABOVE, BELOW = 1, 2
OWN = 24
UNROLL = 16


def rows_needed(height):
    flux = (-ABOVE - 1, height + BELOW)
    need = [{ELEV: (0, height - 1), FIRST: flux, SECOND: flux}]
    for _ in range(2 * STEPS):
        e, f, s = need[0][ELEV], need[0][FIRST], need[0][SECOND]
        need.insert(0, {ELEV: (min(e[0], f[0] - 1, s[0]), max(e[1], f[1] + 1, s[1])), FIRST: (min(f[0], e[0] - 1), max(f[1], e[1] + 1)), SECOND: (min(s[0], e[0]), max(s[1], e[1]))})
    return need


def halo_rows(height):
    need = rows_needed(height)
    past = lambda stage, name: need[stage][name][1] - (height - 1)
    return {ELEV: past(0, ELEV), FIRST: past(0, FIRST), SECOND: past(0, SECOND), FORCE_A: past(1, FIRST), FORCE_B: past(1, SECOND), HALF: past(1, ELEV), DEPTH: past(1, FIRST), LIMITER: BELOW + 1, BED: BELOW, DIFFUSIVITY: BELOW}


AHEAD = (SECOND, FORCE_B, KEEP_AHEAD, WET_AHEAD)
FLOW = (ELEV, FIRST, SECOND, FORCE_A, FORCE_B, HALF)
BASE_NAMES = FLOW + (DEPTH, LIMITER)
DERIVED_NAMES = (KEEP, WET_DEPTH, KEEP_AHEAD, WET_AHEAD, INVERSE)
SPAN = 64


def message(which, last):
    names = FLOW
    if which == 0:
        names = names + (DEPTH, LIMITER)
    if which == last:
        names = names + (BED, DIFFUSIVITY)
    return names


def offsets(names, tiles, height):
    places, at, count = {}, 0, halo_rows(height)
    for name in names:
        places[name] = at
        at += (tiles + (name in AHEAD)) * count[name]
    return places, -(-at // 8) * 8


def lanes_of(tile):
    return pl.ds(pl.multiple_of(tile * LANES, LANES), LANES)


def lane_index():
    return lax.broadcasted_iota(jnp.int32, (8, LANES), 1)


def ahead(here, after):
    return pltpu.roll(jnp.where(lane_index() == 0, after, here), LANES - 1, 1)


def behind(here, before):
    return pltpu.roll(jnp.where(lane_index() == LANES - 1, before, here), 1, 1)


def prepare_kernel(which, last, keys, place_ref, *args):
    n = len(keys)
    hbm = dict(zip(keys, args[:n]))
    args = args[n + bool(which) :]
    across_ref, chip_ref, base_ref = args[:3]
    args = args[3:]
    if which:
        derived_ref, args = args[0], args[1:]
    held = dict(zip(keys, args[:n]))
    second_ref, force_ref, sem = args[n:]
    copies = []
    for slot, key in enumerate(keys):
        source = hbm[key].at[which] if key in (FLOW_IN, FORCING, WET) else hbm[key]
        copies.append(pltpu.make_async_copy(source, held[key], sem.at[slot]))
        copies[-1].start()
    height, tiles = held[DEPTH].shape[0], held[DEPTH].shape[1] // LANES
    names = message(which, last)
    places, _ = offsets(names, tiles, height)
    count = halo_rows(height)
    slot_of = {name: k for k, name in enumerate(BASE_NAMES)}

    zero = jnp.zeros((height, LANES), jnp.float32)
    for ref in (second_ref, force_ref):
        for edge in (0, tiles + 1):
            ref[edge, :, :] = zero
    zero = jnp.zeros((SPAN, LANES), jnp.float32)
    for name in (ELEV, HALF, DEPTH):
        for edge in (0, tiles + 1):
            base_ref[slot_of[name], edge, :, :] = zero
    for copy in copies:
        copy.wait()

    def derive(tile, carry):
        at = tile + 1
        for row in range(0, height, 8):
            rows = slice(row, row + 8)

            def put(name, value):
                base_ref[slot_of[name], at, OWN + row : OWN + row + 8, :] = value

            depth = held[DEPTH][rows, lanes_of(tile)]
            half = (0.5 * time_step) * held[WET][rows, lanes_of(tile)].astype(jnp.float32)
            push = 2.0 * half * depth
            put(ELEV, held[FLOW_IN][0, rows, lanes_of(tile)])
            put(FIRST, depth * held[FLOW_IN][1, rows, lanes_of(tile)])
            put(FORCE_A, push * held[FORCING][0, rows, lanes_of(tile)])
            put(HALF, half)
            put(DEPTH, depth)
            put(LIMITER, held[LIMITER][rows, lanes_of(tile)].astype(jnp.float32))
            second_ref[at, rows, :] = depth * held[FLOW_IN][2, rows, lanes_of(tile)]
            force_ref[at, rows, :] = push * held[FORCING][1, rows, lanes_of(tile)]
        return carry

    lax.fori_loop(0, tiles, derive, 0, unroll=2)

    def shift(block, carry):
        for row in range(0, height, 8):
            rows = slice(row, row + 8)
            for name, ref in ((SECOND, second_ref), (FORCE_B, force_ref)):
                moved = ahead(ref[block, rows, :], ref[block + 1, rows, :])
                base_ref[slot_of[name], block, OWN + row : OWN + row + 8, :] = moved
        return carry

    shift(0, 0)
    lax.fori_loop(1, tiles + 1, shift, 0, unroll=4)

    def fill(head_ref, tail_ref):
        def give(name, block, chunk):
            rows = count[name]
            where = pl.ds(places[name] + chunk * rows, rows)
            if name in slot_of:
                head_ref[where, :] = base_ref[slot_of[name], block, OWN : OWN + rows, :]
                tail_ref[where, :] = base_ref[slot_of[name], block, OWN + height - rows : OWN + height, :]
            else:
                head_ref[where, :] = held[name][:rows, lanes_of(chunk)]
                tail_ref[where, :] = held[name][height - rows :, lanes_of(chunk)]

        def body(tile, carry):
            for name in names:
                give(name, tile + 1, tile + (name in AHEAD))
            return carry

        for name in names:
            if name in AHEAD:
                give(name, 0, 0)
        lax.fori_loop(0, tiles, body, 0, unroll=2)

    odd = place_ref[1]

    @pl.when(odd == 0)
    def _():
        fill(across_ref, chip_ref)

    @pl.when(odd == 1)
    def _():
        fill(chip_ref, across_ref)

    if which:
        derive_kernel(base_ref, derived_ref, height=height)


def derive_rows(base, derived, block, row, names):
    rows = slice(row, row + 8)

    def put(name, value):
        derived[DERIVED_NAMES.index(name), block, rows, :] = value

    half_at, depth_at = BASE_NAMES.index(HALF), BASE_NAMES.index(DEPTH)
    half, depth = base[half_at, block, rows, :], base[depth_at, block, rows, :]
    if KEEP in names:
        put(KEEP, 1.0 - (2.0 * friction) * half)
        put(WET_DEPTH, gravity * half * depth)
    if INVERSE in names:
        put(INVERSE, jnp.where(depth > 0.0, 1.0 / depth, 0.0))
    if KEEP_AHEAD in names:
        half = ahead(half, base[half_at, block + 1, rows, :])
        depth = ahead(depth, base[depth_at, block + 1, rows, :])
        put(KEEP_AHEAD, 1.0 - (2.0 * friction) * half)
        put(WET_AHEAD, gravity * half * depth)


def derive_kernel(base_ref, derived_ref, *, height):
    tiles = base_ref.shape[1] - 2

    def body(block, carry):
        for row in range(OWN, OWN + height, 8):
            derive_rows(base_ref, derived_ref, block, row, DERIVED_NAMES)
        return carry

    body(0, 0)
    lax.fori_loop(1, tiles + 1, body, 0, unroll=2)


def beside(field, tile, rows, centre):
    return behind(centre, field[tile - 1, rows, :]), ahead(centre, field[tile + 1, rows, :])


def flow_kernel(which, last_cond, height, keys, place_ref, weights_ref, *args):
    refs = dict(zip(keys, args))
    n_in = len(keys)
    surface_ref, low_ref, high_ref, base_ref, derived_ref = args[n_in : n_in + 5]
    scratch = (ELEV_MID, FIRST_MID, SECOND_MID, FLUX_A, FLUX_B)
    buf = dict(zip(scratch, args[n_in + 5 : n_in + 5 + len(scratch)]))
    buf.update((name, base_ref.at[k]) for k, name in enumerate(BASE_NAMES))
    buf.update((name, derived_ref.at[k]) for k, name in enumerate(DERIVED_NAMES))
    surface_buf, sem = args[n_in + 5 + len(scratch) :]
    tiles = base_ref.shape[1] - 2
    flow_places, _ = offsets(message(which, last_cond), tiles, height)
    static_places, _ = offsets(message(0, last_cond), tiles, height)
    count, need = halo_rows(height), rows_needed(height)

    zero = jnp.zeros((SPAN, LANES), jnp.float32)
    for name in (ELEV_MID, FLUX_B):
        buf[name][0, :, :] = zero
        buf[name][tiles + 1, :, :] = zero

    def load(head, tail, static_head, static_tail):
        def place(name, block, chunk, top, bottom, places):
            rows = count[name]
            where = pl.ds(places[name] + chunk * rows, rows)
            buf[name][block, OWN - rows : OWN, :] = top[where, :]
            buf[name][block, OWN + height : OWN + height + rows, :] = bottom[where, :]

        def body(tile, carry):
            block = tile + 1
            for name in FLOW:
                place(name, block, tile + (name in AHEAD), head, tail, flow_places)
            for name in (DEPTH, LIMITER):
                place(name, block, tile, static_head, static_tail, static_places)
            return carry

        for name in AHEAD:
            if name in FLOW:
                place(name, 0, 0, head, tail, flow_places)
        lax.fori_loop(0, tiles, body, 0, unroll=2)

    odd = place_ref[1]

    @pl.when(odd == 0)
    def _():
        load(refs[ACROSS], refs[CHIP], refs[STATIC_ACROSS], refs[STATIC_CHIP])

    @pl.when(odd == 1)
    def _():
        load(refs[CHIP], refs[ACROSS], refs[STATIC_CHIP], refs[STATIC_ACROSS])

    def outer(block, carry):
        for row in (OWN - 8, OWN + height):
            derive_rows(base_ref, derived_ref, block, row, DERIVED_NAMES)
        derive_rows(base_ref, derived_ref, block, OWN + height + 8, (KEEP,))
        return carry

    outer(0, 0)
    lax.fori_loop(1, tiles + 1, outer, 0, unroll=4)

    def starts(span_):
        return range(OWN + span_[0], OWN + span_[1] + 1, 8)

    def section(number):
        second = number % 2 == 0
        source = (ELEV_MID, FIRST_MID, SECOND_MID) if second else (ELEV, FIRST, SECOND)
        target = (ELEV, FIRST, SECOND) if second else (ELEV_MID, FIRST_MID, SECOND_MID)
        elev, first, vert = (buf[name] for name in source)
        final = number == 2 * STEPS

        def finish(name, at, rows, value):
            if second:
                value = 0.5 * (buf[name][at, rows, :] + value)
            if not (final and name == ELEV):
                buf[target[(ELEV, FIRST, SECOND).index(name)]][at, rows, :] = value
            return value

        def vertical(at):
            for row in starts(need[number][SECOND]):
                rows = slice(row, row + 8)
                here, after = elev[at, rows, :], elev[at + 1, rows, :]
                beyond = pltpu.roll(jnp.where(lane_index() < 2, after, here), LANES - 2, 1)
                kept = buf[KEEP_AHEAD][at, rows, :] * vert[at, rows, :] + buf[FORCE_B][at, rows, :]
                finish(SECOND, at, rows, kept - buf[WET_AHEAD][at, rows, :] * (beyond - here))

        def body(tile, carry):
            at = tile + 1
            for row in starts(need[number][ELEV]):
                rows, up, down = slice(row, row + 8), slice(row - 1, row + 7), slice(row + 1, row + 9)
                here, before = vert[at, rows, :], vert[at - 1, rows, :]
                back = pltpu.roll(jnp.where(lane_index() >= LANES - 2, before, here), 2, 1)
                gone = (first[at, down, :] - first[at, up, :]) + (here - back)
                value = finish(ELEV, at, rows, elev[at, rows, :] - buf[HALF][at, rows, :] * gone)
                if final:
                    surface_buf[row - OWN : row - OWN + 8, lanes_of(tile)] = value
            for row in starts(need[number][FIRST]):
                rows, up, down = slice(row, row + 8), slice(row - 1, row + 7), slice(row + 1, row + 9)
                kept = buf[KEEP][at, rows, :] * first[at, rows, :] + buf[FORCE_A][at, rows, :]
                finish(FIRST, at, rows, kept - buf[WET_DEPTH][at, rows, :] * (elev[at, down, :] - elev[at, up, :]))
            vertical(at)
            return carry

        vertical(0)
        lax.fori_loop(0, tiles, body, 0, unroll=UNROLL)

    def transports(step):
        def body(tile, carry):
            at = tile + 1
            for row in starts(need[-1][FIRST]):
                rows = slice(row, row + 8)
                inverse = buf[INVERSE][at, rows, :]
                vel_a = buf[FIRST][at, rows, :] * inverse
                vel_b = behind(buf[SECOND][at, rows, :], buf[SECOND][at - 1, rows, :]) * inverse
                energy = vel_a * vel_a + vel_b * vel_b
                factor = (transport_base + energy) / (1.0 + buf[LIMITER][at, rows, :] * energy)
                flux_a, flux_b = vel_a * factor, vel_b * factor
                if step:
                    flux_a = buf[FLUX_A][at, rows, :] + flux_a
                    flux_b = buf[FLUX_B][at, rows, :] + flux_b
                buf[FLUX_A][at, rows, :] = flux_a
                buf[FLUX_B][at, rows, :] = flux_b
            return carry

        lax.fori_loop(0, tiles, body, 0, unroll=UNROLL)

    for step in range(STEPS):
        section(2 * step + 1)
        section(2 * step + 2)
        if step == STEPS - 1:
            store = pltpu.make_async_copy(surface_buf, surface_ref.at[which], sem)
            store.start()
        transports(step)

    total = weights_ref[0]
    for other in range(1, weights_ref.shape[0]):
        total = total + weights_ref[other]
    scale = jnp.full((8, LANES), weights_ref[place_ref[0] + which], jnp.int32).astype(jnp.float32)
    scale = (-0.5 * morph_factor) * scale / jnp.full((8, LANES), total, jnp.int32).astype(jnp.float32)
    reach = height + ABOVE + BELOW
    begins = list(range(0, reach - 7, 8))
    if begins[-1] + 8 < reach:
        begins.append(reach - 8)

    def emit(out_ref, before, start):
        def body(local_tile, carry):
            at = start + local_tile + 1
            for begin in begins:
                row = OWN - ABOVE + begin
                rows, up, down = slice(row, row + 8), slice(row - 1, row + 7), slice(row + 1, row + 9)
                left, right = beside(buf[FLUX_B], at, rows, buf[FLUX_B][at, rows, :])
                change = (buf[FLUX_A][at, down, :] - buf[FLUX_A][at, up, :]) + (right - left)
                where = pl.ds(local_tile * reach + begin, 8)
                piece = scale * change
                if before is not None:
                    piece = before[where, :] + piece
                out_ref[where, :] = piece
            return carry

        lax.fori_loop(0, tiles // 2, body, 0, unroll=UNROLL)

    emit(low_ref, refs.get(LOW), 0)
    emit(high_ref, refs.get(HIGH), tiles // 2)
    store.wait()


FIELD = 8


def faces_kernel(last, place_ref, bed_ref, diffuse_ref, across_ref, chip_ref, _, faces_ref, wide):
    height, tiles = bed_ref.shape[0], bed_ref.shape[1] // LANES
    places, _ = offsets(message(last, last), tiles, height)
    count = halo_rows(height)
    zero = jnp.zeros(wide.shape[1:], jnp.float32)
    wide[0, :, :] = zero
    wide[tiles + 1, :, :] = zero

    def load(head, tail):
        def body(tile, carry):
            for name, dst, block, ref in ((BED, faces_ref.at[0], tile, bed_ref), (DIFFUSIVITY, wide, tile + 1, diffuse_ref)):
                rows = count[name]
                where = pl.ds(places[name] + tile * rows, rows)
                dst[block, FIELD - rows : FIELD, :] = head[where, :]
                for row in range(0, height, 8):
                    dst[block, FIELD + row : FIELD + row + 8, :] = ref[row : row + 8, lanes_of(tile)]
                dst[block, FIELD + height : FIELD + height + rows, :] = tail[where, :]
            return carry

        lax.fori_loop(0, tiles, body, 0, unroll=2)

    odd = place_ref[1]

    @pl.when(odd == 0)
    def _():
        load(across_ref, chip_ref)

    @pl.when(odd == 1)
    def _():
        load(chip_ref, across_ref)

    def face(here, there):
        both = here + there
        return jnp.where(both > 0.0, slope_coeff * here * there / both, 0.0)

    def body(tile, carry):
        at = tile + 1
        for row in range(FIELD, FIELD + height + 1, 8):
            rows, up = slice(row, row + 8), slice(row - 1, row + 7)
            here = wide[at, rows, :]
            left, right = beside(wide, at, rows, here)
            faces_ref[1, tile, up, :] = face(wide[at, up, :], here)
            faces_ref[2, tile, rows, :] = face(here, right)
            faces_ref[3, tile, rows, :] = face(here, left)
        return carry

    lax.fori_loop(0, tiles, body, 0, unroll=2)


def moment_kernel(faces_ref, low_ref, low_other_ref, high_ref, high_other_ref, rhs_ref, image_ref, moments_ref, field, image):
    tiles, height = rhs_ref.shape[:2]
    reach = height + ABOVE + BELOW
    zero = jnp.zeros(field.shape[1:], jnp.float32)
    for scratch in (field, image):
        scratch[0, :, :] = zero
        scratch[tiles + 1, :, :] = zero
    begins = list(range(0, reach - 7, 8))
    if begins[-1] + 8 < reach:
        begins.append(reach - 8)

    def add(mine, other, start):
        def body(local_tile, carry):
            for begin in begins:
                where = pl.ds(local_tile * reach + begin, 8)
                rows = slice(FIELD - ABOVE + begin, FIELD - ABOVE + begin + 8)
                tile = start + local_tile
                field[tile + 1, rows, :] = faces_ref[0, tile, rows, :] + (mine[where, :] + other[where, :])
            return carry

        lax.fori_loop(0, tiles // 2, body, 0, unroll=True)

    add(low_ref, low_other_ref, 0)
    add(high_ref, high_other_ref, tiles // 2)

    def apply(tile, carry):
        at = tile + 1
        square, first = carry
        for row in range(FIELD, FIELD + height + 1, 8):
            rows, up, down = slice(row, row + 8), slice(row - 1, row + 7), slice(row + 1, row + 9)
            x = field[at, rows, :]
            left, right = beside(field, at, rows, x)
            gap_down, gap_right = x - field[at, down, :], x - right
            flow_down, flow_right = faces_ref[1, tile, rows, :] * gap_down, faces_ref[2, tile, rows, :] * gap_right
            result = (flow_down + faces_ref[1, tile, up, :] * (x - field[at, up, :])) + (
                flow_right + faces_ref[3, tile, rows, :] * (x - left)
            )
            image[at, rows, :] = result
            if row < FIELD + height:
                rhs_ref[tile, row - FIELD : row - FIELD + 8, :] = x
                image_ref[tile, row - FIELD : row - FIELD + 8, :] = result
                square = square + x * x
                first = first + (flow_down * gap_down + flow_right * gap_right)
        return square, first

    zero = jnp.zeros((8, LANES), jnp.float32)
    square, first = lax.fori_loop(0, tiles, apply, (zero, zero), unroll=True)

    def again(tile, carry):
        at = tile + 1
        second, third = carry
        for row in range(FIELD, FIELD + height, 8):
            rows, down = slice(row, row + 8), slice(row + 1, row + 9)
            w = image[at, rows, :]
            gap_down, gap_right = w - image[at, down, :], w - ahead(w, image[at + 1, rows, :])
            second = second + w * w
            third = third + (
                faces_ref[1, tile, rows, :] * (gap_down * gap_down) + faces_ref[2, tile, rows, :] * (gap_right * gap_right)
            )
        return second, third

    second, third = lax.fori_loop(0, tiles, again, (zero, zero), unroll=True)
    for slot, value in enumerate((square, first, second, third)):
        moments_ref[slot : slot + 1, :] = jnp.sum(value, axis=0, keepdims=True)
    moments_ref[4:8, :] = jnp.zeros((4, LANES), jnp.float32)


def final_kernel(rhs_ref, image_ref, *args):
    moments, (out_ref,) = args[:-1], args[-1:]
    total = moments[0][...]
    for part in moments[1:]:
        total = total + part[...]
    total = jnp.sum(total, axis=1, keepdims=True)
    norm, first, second, third = (total[slot : slot + 1, :] for slot in range(4))
    alpha = norm / (norm + first)
    theta = first / norm
    spread_ = second - theta * first
    curve = third - 2.0 * theta * second + theta * theta * first
    ratio = alpha * alpha * spread_ / norm
    beta = spread_ / (spread_ + curve - alpha * spread_ * (spread_ / norm))
    on_rhs = jnp.broadcast_to(alpha + beta * (alpha * theta + ratio), (8, LANES))
    on_image = jnp.broadcast_to(beta * alpha, (8, LANES))
    tiles, height = rhs_ref.shape[:2]

    def body(tile, carry):
        for row in range(0, height, 8):
            rows = slice(row, row + 8)
            out_ref[rows, lanes_of(tile)] = on_rhs * rhs_ref[tile, rows, :] - on_image * image_ref[tile, rows, :]
        return carry

    lax.fori_loop(0, tiles, body, 0, unroll=4)


SMEM = pl.BlockSpec(memory_space=pltpu.SMEM)
PARAMS = dict(vmem_limit_bytes=32 * 1024 * 1024)


def cost(flops, moved):
    return pl.CostEstimate(flops=flops, bytes_accessed=moved, transcendentals=0)


def swap_chip(x, count):
    return lax.ppermute(x, "space", [(i, i ^ 1) for i in range(count)])


def swap_across(x, count):
    pairs = [(i, i + 1) for i in range(1, count - 1, 2)]
    return lax.ppermute(x, "space", pairs + [(b, a) for a, b in pairs])


def phases_of(count):
    bits = [1 << k for k in range(count.bit_length() - 1)]
    out = [bits[:1]]
    for k in range(1, len(bits), 2):
        pair = bits[k : k + 2]
        out.append([pair[0]] if len(pair) == 1 else [pair[0], pair[1], pair[0] + pair[1]])
    return out


def local(flow, forcing, wet, depth, limiter, weights, bed, diffusivity):
    here, _, height, width = flow.shape
    bed_here, diffuse_here = bed, diffusivity
    flow, forcing, wet, depth, limiter, bed, diffusivity = (
        pltpu.with_memory_space_constraint(v, pltpu.HBM) for v in (flow, forcing, wet, depth, limiter, bed, diffusivity)
    )
    tiles = width // LANES
    strips, groups = lax.axis_size("space"), lax.axis_size("cond")
    place = jnp.stack([lax.axis_index("cond") * here, lax.axis_index("space") % 2]).astype(jnp.int32)
    reach = height + ABOVE + BELOW

    last = here - 1
    local_vmem = pl.BlockSpec(memory_space=pltpu.VMEM)
    anywhere = pl.BlockSpec(memory_space=pltpu.HBM)
    base_shape = jax.ShapeDtypeStruct((len(BASE_NAMES), tiles + 2, SPAN, LANES), jnp.float32)
    derived_shape = jax.ShapeDtypeStruct((len(DERIVED_NAMES), tiles + 2, SPAN, LANES), jnp.float32)

    across, chip, base, derived = [], [], [], []
    for which in range(here):
        arrays = {FLOW_IN: flow, FORCING: forcing, WET: wet, DEPTH: depth, LIMITER: limiter}
        if which == last:
            arrays.update({BED: bed, DIFFUSIVITY: diffusivity})
        keys = tuple(arrays)
        size = offsets(message(which, last), tiles, height)[1]
        shape = jax.ShapeDtypeStruct((size, LANES), jnp.float32)
        held = [pltpu.VMEM(v.shape[1:] if k in (FLOW_IN, FORCING, WET) else v.shape, v.dtype) for k, v in arrays.items()]
        out = pl.pallas_call(
            functools.partial(prepare_kernel, which, last, keys),
            out_shape=(shape, shape, base_shape) + (derived_shape,) * bool(which),
            in_specs=[SMEM] + [anywhere] * len(keys) + [pl.BlockSpec(memory_space=pl.ANY)] * bool(which),
            out_specs=(local_vmem,) * (3 + bool(which)),
            scratch_shapes=held
            + [pltpu.VMEM((tiles + 2, height, LANES), jnp.float32)] * 2
            + [pltpu.SemaphoreType.DMA((len(keys),))],
            compiler_params=pltpu.CompilerParams(**PARAMS),
            cost_estimate=cost(1000, 8 * height * width * 4 + size * LANES * 8),
            name=f"prepare{which}",
        )(place, *arrays.values(), *derived[-1:])
        across.append(swap_across(out[0], strips))
        chip.append(swap_chip(out[1], strips))
        base.append(out[2])
        if which:
            derived.append(out[3])
        else:
            derived.append(
                pl.pallas_call(
                    functools.partial(derive_kernel, height=height),
                    out_shape=derived_shape,
                    in_specs=[local_vmem],
                    out_specs=local_vmem,
                    compiler_params=pltpu.CompilerParams(**PARAMS),
                    cost_estimate=cost(1000, 7 * height * width * 4),
                    name="derive",
                )(out[2])
            )

    surface_shape = jax.ShapeDtypeStruct((here, height, width), jnp.float32)
    half_shape = jax.ShapeDtypeStruct((tiles // 2 * reach, LANES), jnp.float32)
    surface = low = high = None
    for which in range(here):
        arrays = {ACROSS: across[which], CHIP: chip[which], STATIC_ACROSS: across[0], STATIC_CHIP: chip[0]}
        if which:
            arrays.update({LOW: low, HIGH: high})
        arrays.update({BASE: base[which], DERIVED: derived[which]})
        specs = [local_vmem] * len(arrays)
        aliases = {len(arrays): 3, len(arrays) + 1: 4}
        if which:
            arrays[SURFACE] = surface
            specs.append(anywhere)
            aliases[1 + len(arrays)] = 0
        keys = tuple(arrays)
        surface, low, high, _, _ = pl.pallas_call(
            functools.partial(flow_kernel, which, last, height, keys),
            out_shape=(surface_shape, half_shape, half_shape, base_shape, derived_shape),
            in_specs=[SMEM, SMEM] + specs,
            out_specs=(anywhere,) + (local_vmem,) * 4,
            scratch_shapes=[pltpu.VMEM((tiles + 2, SPAN, LANES), jnp.float32)] * 5
            + [pltpu.VMEM((height, width), jnp.float32), pltpu.SemaphoreType.DMA],
            input_output_aliases=aliases,
            compiler_params=pltpu.CompilerParams(**PARAMS),
            cost_estimate=cost(2 * STEPS * 40 * 40 * width, 8 * height * width * 4),
            name=f"flow{which}",
        )(place, weights, *arrays.values())

    faces = pl.pallas_call(
        functools.partial(faces_kernel, last),
        out_shape=jax.ShapeDtypeStruct((4, tiles, height + 24, LANES), jnp.float32),
        in_specs=[SMEM] + [local_vmem] * 4 + [pl.BlockSpec(memory_space=pl.ANY)],
        out_specs=local_vmem,
        scratch_shapes=[pltpu.VMEM((tiles + 2, height + 24, LANES), jnp.float32)],
        compiler_params=pltpu.CompilerParams(**PARAMS),
        cost_estimate=cost(60 * height * width, 8 * height * width * 4),
        name="faces",
    )(place, bed_here, diffuse_here, across[last], chip[last], low)

    bits = [1 << k for k in range(groups.bit_length() - 1)]
    for k, bit in enumerate(bits):
        low_other = lax.ppermute(low, "cond", [(i, i ^ bit) for i in range(groups)])
        flip = bits[-1 - k]
        high_other = lax.ppermute(high, "cond", [(i, i ^ flip) for i in range(groups)])
        if k + 1 < len(bits):
            low, high = low + low_other, high + high_other

    block = jax.ShapeDtypeStruct((tiles, height, LANES), jnp.float32)
    small = jax.ShapeDtypeStruct((8, LANES), jnp.float32)
    wide = pltpu.VMEM((tiles + 2, height + 24, LANES), jnp.float32)
    rhs, image, moments = pl.pallas_call(
        moment_kernel,
        out_shape=(block, block, small),
        in_specs=[local_vmem] * 5,
        out_specs=(local_vmem,) * 3,
        scratch_shapes=[wide] * 2,
        compiler_params=pltpu.CompilerParams(**PARAMS),
        cost_estimate=cost(60 * height * width, 8 * height * width * 4),
        name="moments",
    )(faces, low, low_other, high, high_other)

    phases = phases_of(strips)
    for k, phase in enumerate(phases):
        others = [lax.ppermute(moments, "space", [(i, i ^ m) for i in range(strips)]) for m in phase]
        if k + 1 < len(phases):
            for other in others:
                moments = moments + other

    terms = [moments] + others
    bed_new = pl.pallas_call(
        final_kernel,
        out_shape=jax.ShapeDtypeStruct((height, width), jnp.float32),
        in_specs=[local_vmem] * (2 + len(terms)),
        out_specs=local_vmem,
        compiler_params=pltpu.CompilerParams(**PARAMS),
        cost_estimate=cost(3 * height * width, 3 * height * width * 4),
        name="final",
    )(rhs, image, *terms)
    return (surface, bed_new)


def solution(mesh):
    in_specs = (
        P("cond", None, "space", None),
        P("cond", None, "space", None),
        P("cond", "space", None),
        P("space", None),
        P("space", None),
        P(),
        P("space", None),
        P("space", None),
    )
    out_specs = (P("cond", "space", None), P("space", None))
    return jax.shard_map(local, mesh=mesh, in_specs=in_specs, out_specs=out_specs, check_vma=False)
```
